32 devices in a mesh: brick: 16 (over z, y, x), shard: 2 (over core).
Axes of the slice: x: 2, y: 2, z: 4, core: 2. Of those that a mesh axis runs over, the one named last changes fastest.
Arguments:
- velocity: float32 [3, 16, 16384], P(None, 'brick', 'shard'), may hold values from -6 to 6
- particle_mass: float32 [16, 16384], P('brick', 'shard'), may hold values from 0.5 to 2
- particle_volume: float32 [16, 16384], P('brick', 'shard'), may hold values from 0.5 to 2
- lame_first: float32 [16, 16384], P('brick', 'shard'), may hold values from 0.5 to 2
- shear_modulus: float32 [16, 16384], P('brick', 'shard'), may hold values from 0.25 to 1
- stress: float32 [6, 16, 16384], P(None, 'brick', 'shard'), may hold values from -6 to 6
- corner_weights: bfloat16 [16, 128, 64, 128], P('brick', 'shard'), may hold values from 0 to 0.0625
- corner_grads: bfloat16 [3, 16, 128, 64, 128], P(None, 'brick', 'shard'), may hold values from -0.375 to 0.375
- tile_block: int32 [16, 128], P('brick', 'shard'), may hold values from 0 to 255, as said below
- face_blocks: int32 [16, 4, 16], P('brick'), may hold values from 0 to 255, as said below
Outputs:
- new_velocity: float32 [3, 16, 16384], P(None, 'brick', 'shard')
- new_stress: float32 [6, 16, 16384], P(None, 'brick', 'shard')
The draws below stay inside these ranges and needn't reach their ends.
Inputs may be any that keep to these rules, and one draw needn't show every extreme that they name: Within one brick the 4 x 16 entries are distinct node blocks, and face_blocks[b, k, f] lies among the 16 consecutive node blocks that begin at f * 16. `tile_block`: within one brick the tiles touch min(256, 112) distinct node blocks, among them as many of the face_blocks entries of the brick as that count allows; the other tiles touch blocks of that set again.
All inputs are finite; a program needn't handle non-finite values.
Results may differ from the reference program's by a relative error of at most 0.0011.
Values may be sent and summed in bfloat16 or wider, within the bound.
A program may use at most 64 MiB of HBM per device.

```python
import math
import jax
import jax.numpy as jnp
import numpy as np
from jax import lax

BLK = 64
TP = 128
NB = 256
CUTS = 4
FB = 16
NBRICK = 16
TILES = 128
PART = 16384


def brick_layout(key):
    group = NB // FB
    body_count = min(NB, TILES - TILES // 8)

    def single_brick(single):
        keys = jax.random.split(single, 4)
        group_keys = jax.random.split(keys[0], FB)
        picks = jax.vmap(lambda group_key: jax.random.permutation(group_key, group)[:CUTS])(group_keys)
        faces = jnp.transpose(picks.astype(jnp.int32) + group * jnp.arange(FB, dtype=jnp.int32)[:, None])
        on_face = jnp.zeros((NB,), jnp.int32).at[faces.reshape(-1)].set(1)
        ranks = jax.random.permutation(keys[1], NB).astype(jnp.int32)
        scores = ranks + NB * (1 - on_face)
        order = jnp.argsort(scores, stable=True).astype(jnp.int32)
        body_blocks = order[:body_count]
        extra_index = jax.random.randint(keys[2], (TILES - body_count,), 0, body_count)
        tiles = jnp.concatenate([body_blocks, body_blocks[extra_index]])
        tiles = tiles[jax.random.permutation(keys[3], TILES)]
        return (faces.astype(jnp.int32), tiles.astype(jnp.int32))
    return jax.vmap(single_brick)(jax.random.split(key, NBRICK))


def draw_face_blocks(key, part):
    faces, tiles = brick_layout(jax.random.fold_in(key, 7))
    return faces


def draw_tile_block(key, part):
    faces, tiles = brick_layout(jax.random.fold_in(key, 7))
    return tiles


def draw_corner_weights(key, part):
    base_key = jax.random.fold_in(key, 11)
    scale_key = jax.random.fold_in(key, 13)
    base = jax.random.uniform(base_key, (NBRICK, TILES, BLK, TP), jnp.float32, 0.0, 0.03125)
    tile_scale = jnp.exp(jax.random.uniform(scale_key, (NBRICK, TILES, 1, 1), jnp.float32, jnp.log(0.125), jnp.log(2.0)))
    return (base * tile_scale).astype(jnp.bfloat16)


def steps_of(stream_key, shape, cuts, low, largest):
    gain, own = 1.0, jax.random.fold_in(stream_key, 6)
    for position, blocks in cuts:
        steps = jnp.exp(jax.random.uniform(jax.random.fold_in(own, position), (blocks,), jnp.float32, low / len(cuts), largest / len(cuts)))
        gain = gain * jnp.repeat(steps, shape[position] // blocks).reshape([-1 if axis == position else 1 for axis in range(len(shape))])
    return gain


def gaussian(rng, extent, spread, reach, cuts=(), kind=jnp.bfloat16):
    values = spread * jax.random.normal(rng, extent, jnp.float32)
    if cuts:
        values = values * steps_of(rng, extent, cuts, -0.22, 0.18)
    return jnp.clip(values, -reach, reach).astype(kind)


def setup_inputs(seed: int = 0) -> dict:
    arg_keys = jax.random.split(jax.random.key(seed), 11)
    return {
        "velocity": gaussian(arg_keys[0], (3, NBRICK, PART), 1.0, 6.0, ((1, 16), (2, 2)), jnp.float32),
        "particle_mass": jnp.clip(jnp.exp(math.log(2.0) - 1.3862944 * jax.random.uniform(arg_keys[1], (NBRICK, PART), jnp.float32) ** steps_of(arg_keys[1], (NBRICK, PART), ((0, 16), (1, 2)), -0.2, 0.2)), 0.5, 2.0),
        "particle_volume": jnp.clip(jnp.exp(math.log(2.0) - 1.3862944 * jax.random.uniform(arg_keys[2], (NBRICK, PART), jnp.float32) ** steps_of(arg_keys[2], (NBRICK, PART), ((0, 16), (1, 2)), -0.2, 0.2)), 0.5, 2.0),
        "lame_first": jnp.clip(jnp.exp(math.log(2.0) - 1.3862944 * jax.random.uniform(arg_keys[3], (NBRICK, PART), jnp.float32) ** steps_of(arg_keys[3], (NBRICK, PART), ((0, 16), (1, 2)), -0.2, 0.2)), 0.5, 2.0),
        "shear_modulus": jnp.clip(jnp.exp(math.log(1.0) - 1.3862944 * jax.random.uniform(arg_keys[4], (NBRICK, PART), jnp.float32) ** steps_of(arg_keys[4], (NBRICK, PART), ((0, 16), (1, 2)), -0.2, 0.2)), 0.25, 1.0),
        "stress": gaussian(arg_keys[5], (6, NBRICK, PART), 1.0, 6.0, ((1, 16), (2, 2)), jnp.float32),
        "corner_weights": draw_corner_weights(jax.random.fold_in(arg_keys[10], 71), 0),
        "corner_grads": gaussian(arg_keys[7], (3, NBRICK, TILES, BLK, TP), 0.0625, 0.375, ((1, 16), (2, 2))),
        "tile_block": draw_tile_block(jax.random.fold_in(arg_keys[10], 71), 0),
        "face_blocks": draw_face_blocks(jax.random.fold_in(arg_keys[10], 71), 0),
    }


STEP = 0.5
FLOOR = 1.0


def particle_terms(velocity, particle_mass, particle_volume, stress):
    loads = jnp.concatenate([particle_mass[None], particle_mass[None] * velocity], 0).astype(jnp.bfloat16)
    pairing = np.array([[0, 3, 5], [3, 1, 4], [5, 4, 2]])
    scaled = (particle_volume[None, None] * stress[pairing]).astype(jnp.bfloat16)
    return loads, scaled


def tile_sums(loads, scaled, weights, grads, blocks):
    tile_count, block_nodes, tile_parts = weights.shape
    loads_tiled = loads.reshape(4, tile_count, tile_parts).astype(jnp.float32)
    scaled_tiled = scaled.reshape(3, 3, tile_count, tile_parts).astype(jnp.float32)
    weights_wide = weights.astype(jnp.float32)
    grads_wide = grads.astype(jnp.float32)
    terms = jnp.einsum('ctp,tnp->tcn', loads_tiled, weights_wide)
    force = jnp.einsum('ijtp,jtnp->tin', scaled_tiled, grads_wide)
    pieces = jnp.concatenate([terms[:, :1], terms[:, 1:] - STEP * force], 1)
    pieces = pieces.reshape(tile_count, 4 * block_nodes)
    return jax.ops.segment_sum(pieces, blocks, num_segments=NB)


def update_nodes(grid, block_ids, rooted):
    rows_here = grid.shape[0]
    block_nodes = grid.shape[1] // 4
    node_mass = grid[:, :block_nodes]
    moment = grid[:, block_nodes:].reshape(rows_here, 3, block_nodes)
    gravity = jnp.array([0.0, 0.0, -1.0], jnp.float32)
    moment = moment + STEP * node_mass[:, None, :] * gravity[None, :, None]
    speeds = moment / jnp.maximum(node_mass, FLOOR)[:, None, :]
    fixed = jnp.logical_and(rooted, block_ids < NB // 8)
    speeds = jnp.where(fixed[:, None, None], jnp.float32(0.0), speeds)
    return speeds.astype(jnp.bfloat16).reshape(rows_here, 3 * block_nodes)


def gather_back(speeds, weights, grads, blocks, stress, lame_first, shear_modulus):
    tile_count, block_nodes, tile_parts = weights.shape
    picked = speeds[blocks].reshape(tile_count, 3, block_nodes).astype(jnp.float32)
    moved = jnp.einsum('tcn,tnp->ctp', picked, weights.astype(jnp.float32)).reshape(3, -1)
    grad_vel = jnp.einsum('tin,jtnp->ijtp', picked, grads.astype(jnp.float32)).reshape(3, 3, -1)
    strain = 0.5 * (grad_vel + jnp.transpose(grad_vel, (1, 0, 2)))
    trace_rate = strain[0, 0] + strain[1, 1] + strain[2, 2]
    rate_six = strain[np.array([0, 1, 2, 0, 1, 0]), np.array([0, 1, 2, 1, 2, 2])]
    identity_six = jnp.array([1.0, 1.0, 1.0, 0.0, 0.0, 0.0], jnp.float32)
    updated = stress + STEP * (lame_first[None] * trace_rate[None] * identity_six[:, None] + 2.0 * shear_modulus[None] * rate_six)
    return moved, updated


def reference(velocity, particle_mass, particle_volume, lame_first, shear_modulus, stress, corner_weights, corner_grads, tile_block, face_blocks):
    def scatter_brick(brick_index):
        loads, scaled = particle_terms(velocity[:, brick_index], particle_mass[brick_index], particle_volume[brick_index], stress[:, brick_index])
        return tile_sums(loads, scaled, corner_weights[brick_index], corner_grads[:, brick_index], tile_block[brick_index])

    grid = lax.map(scatter_brick, jnp.arange(NBRICK))
    brick_rows = jnp.arange(NBRICK)[:, None]
    additions = []
    for cut_index in range(CUTS):
        chosen = face_blocks[:, cut_index]
        facing = grid[brick_rows, chosen]
        partner = np.arange(NBRICK) ^ (1 << cut_index)
        additions.append((chosen, facing[partner]))
    for chosen, incoming in additions:
        grid = grid.at[brick_rows, chosen].add(incoming)
    rooted = jnp.arange(NBRICK) == 0
    block_ids = jnp.arange(NB)
    speeds = jax.vmap(lambda single, flag: update_nodes(single, block_ids, flag))(grid, rooted)

    def return_brick(brick_index):
        return gather_back(speeds[brick_index], corner_weights[brick_index], corner_grads[:, brick_index], tile_block[brick_index], stress[:, brick_index], lame_first[brick_index], shear_modulus[brick_index])

    moved, updated = lax.map(return_brick, jnp.arange(NBRICK))
    return jnp.transpose(moved, (1, 0, 2)), jnp.transpose(updated, (1, 0, 2))
```

```python
import functools

import jax
import jax.numpy as jnp
from jax import lax
from jax.experimental import pallas as pl
from jax.experimental.pallas import tpu as pltpu
from jax.sharding import PartitionSpec as P

NB = 256
STEP = 0.5
FLOOR = 1.0
MESH = pl.DeviceIdType.MESH
GROUP = 8
PAIRING = ((0, 3, 5), (3, 1, 4), (5, 4, 2))
SIX = ((0, 0), (1, 1), (2, 2), (0, 1), (1, 2), (0, 2))


def thirds(value):
    high = value.astype(jnp.bfloat16)
    rest = value - high.astype(jnp.float32)
    middle = rest.astype(jnp.bfloat16)
    low = (rest - middle.astype(jnp.float32)).astype(jnp.bfloat16)
    return jnp.concatenate([high, middle, low], 1)


def select_sum(chosen, value):
    wide = value.shape[1]
    out = jnp.dot(chosen, thirds(value), preferred_element_type=jnp.float32)
    return out[:, :wide] + out[:, wide : 2 * wide] + out[:, 2 * wide :]


def column_of(row):
    size = row.shape[1]
    square = jnp.broadcast_to(row, (size, size))
    rows = lax.broadcasted_iota(jnp.int32, (size, size), 0)
    columns = lax.broadcasted_iota(jnp.int32, (size, size), 1)
    return jnp.sum(jnp.where(rows == columns, square, 0.0), axis=1, keepdims=True)


def row_of(column):
    size = column.shape[0]
    square = jnp.broadcast_to(column, (size, size))
    rows = lax.broadcasted_iota(jnp.int32, (size, size), 0)
    columns = lax.broadcasted_iota(jnp.int32, (size, size), 1)
    return jnp.sum(jnp.where(rows == columns, square, 0.0), axis=0, keepdims=True)


def equal(column, row):
    return jnp.where(column == row, 1.0, 0.0).astype(jnp.bfloat16)


def kernel(
    velocity,
    mass,
    volume,
    lame,
    shear,
    stress,
    weights_in,
    grads_in,
    blocks,
    faces,
    moved_out,
    stress_out,
    weights,
    grads,
    own_sums,
    face_sums,
    other_sums,
    other_blocks,
    face_in,
    load_sem,
    sum_sems,
    block_sems,
    face_send,
    face_recv,
):
    brick = lax.axis_index("brick")
    shard = lax.axis_index("shard")
    tiles, nodes, parts = weights.shape
    cuts, face_count = faces.shape
    groups = tiles // GROUP

    loads = []
    for g in range(groups):
        rows = pl.ds(g * GROUP, GROUP)
        pair = (
            pltpu.make_async_copy(weights_in.at[rows], weights.at[rows], load_sem.at[g, 0]),
            pltpu.make_async_copy(grads_in.at[:, rows], grads.at[:, rows], load_sem.at[g, 1]),
        )
        for copy in pair:
            copy.start()
        loads.append(pair)

    sibling = (brick, 1 - shard)
    partners = []
    for k in range(cuts):
        bit = 2**k
        partner = brick + (1 - 2 * ((brick // bit) % 2)) * bit
        partners.append(((partner, shard), (partner, 1 - shard)))
    barrier = pltpu.get_barrier_semaphore()
    greeted = [sibling] + [device for both in partners for device in both]
    for device in greeted:
        pl.semaphore_signal(barrier, inc=1, device_id=device, device_id_type=MESH)

    lanes = lax.broadcasted_iota(jnp.int32, (GROUP, GROUP * nodes), 1)
    sublanes = lax.broadcasted_iota(jnp.int32, (GROUP, GROUP * nodes), 0)
    own_node = lanes // nodes == sublanes
    width = 2 * nodes

    block_row = blocks[...].astype(jnp.float32)
    block_column = column_of(block_row)
    face_rows = faces[...].astype(jnp.float32)
    face_column = jnp.concatenate([column_of(face_rows[k : k + 1]) for k in range(cuts)], 0)
    face_row = row_of(face_column)
    face_of_tile = equal(block_column, face_row)
    tile_of_face = equal(face_column, block_row)
    same_here = equal(block_column, block_row)

    first_half = lax.broadcasted_iota(jnp.int32, (GROUP, width), 1) < nodes
    for g in range(groups):
        rows = pl.ds(g * GROUP, GROUP)
        for copy in loads[g]:
            copy.wait()
        m = mass[rows]
        zero = jnp.zeros_like(m)
        columns = [jnp.concatenate([m] + [m * velocity[c, rows] for c in range(3)], 0)]
        vol = volume[rows]
        scaled = [(-STEP) * (vol * stress[s, rows]) for s in range(6)]
        for j in range(3):
            columns.append(jnp.concatenate([zero] + [scaled[PAIRING[i][j]] for i in range(3)], 0))
        left = jnp.concatenate([column.astype(jnp.bfloat16) for column in columns], 1)
        right = jnp.concatenate(
            [weights[rows].reshape(GROUP * nodes, parts)]
            + [grads[j, rows].reshape(GROUP * nodes, parts) for j in range(3)],
            1,
        )
        out = lax.dot_general(
            left, right, (((1,), (1,)), ((), ())), preferred_element_type=jnp.float32
        )
        twice = []
        for c in range(4):
            piece = jnp.where(own_node, out[c * GROUP : (c + 1) * GROUP], 0.0)
            total = piece[:, :width]
            for q in range(1, GROUP // 2):
                total = total + piece[:, q * width : (q + 1) * width]
            twice.append(total + pltpu.roll(total, nodes, 1))
        own_sums[rows, :width] = jnp.where(first_half, twice[0], twice[1])
        own_sums[rows, width:] = jnp.where(first_half, twice[2], twice[3])

    pieces = own_sums[...]
    face_sums[...] = select_sum(tile_of_face, pieces)

    pl.semaphore_wait(barrier, len(greeted))
    copies = [
        pltpu.make_async_remote_copy(
            src_ref=own_sums,
            dst_ref=other_sums,
            send_sem=sum_sems.at[0],
            recv_sem=sum_sems.at[1],
            device_id=sibling,
            device_id_type=MESH,
        ),
        pltpu.make_async_remote_copy(
            src_ref=blocks,
            dst_ref=other_blocks,
            send_sem=block_sems.at[0],
            recv_sem=block_sems.at[1],
            device_id=sibling,
            device_id_type=MESH,
        ),
    ]
    for k in reversed(range(cuts)):
        for r in range(2):
            rows = pl.ds(k * face_count, face_count)
            copies.append(
                pltpu.make_async_remote_copy(
                    src_ref=face_sums.at[rows],
                    dst_ref=face_in.at[r, rows],
                    send_sem=face_send.at[r, k],
                    recv_sem=face_recv.at[r, k],
                    device_id=partners[k][r],
                    device_id_type=MESH,
                )
            )
    for copy in copies:
        copy.start()
    total = select_sum(same_here, pieces)
    copies[0].wait()
    copies[1].wait()
    same_there = equal(block_column, other_blocks[...].astype(jnp.float32))
    total = total + select_sum(same_there, other_sums[...])
    for copy in copies[2:]:
        copy.wait()
    total = total + select_sum(face_of_tile, face_in[0] + face_in[1])

    half = lax.broadcasted_iota(jnp.int32, (tiles, width), 1) < nodes
    one, two = total[:, :width], total[:, width:]
    one_turned, two_turned = pltpu.roll(one, nodes, 1), pltpu.roll(two, nodes, 1)
    node_mass = jnp.where(half, one, one_turned)
    moment = [
        jnp.where(half, one_turned, one),
        jnp.where(half, two, two_turned),
        jnp.where(half, two_turned, two) - STEP * node_mass,
    ]
    floor = jnp.maximum(node_mass, FLOOR)
    bound = jnp.where(brick == 0, float(NB // 8), 0.0)
    fixed = block_column < bound
    speeds = [jnp.where(fixed, 0.0, q / floor) for q in moment]

    for g in range(groups):
        rows = pl.ds(g * GROUP, GROUP)
        left = jnp.concatenate(
            [
                jnp.where(
                    own_node,
                    jnp.concatenate([s[g * GROUP : (g + 1) * GROUP]] * (GROUP // 2), 1),
                    0.0,
                )
                for s in speeds
            ],
            0,
        ).astype(jnp.bfloat16)
        right = jnp.concatenate(
            [weights[rows].reshape(GROUP * nodes, parts)]
            + [grads[j, rows].reshape(GROUP * nodes, parts) for j in range(3)],
            1,
        )
        out = jnp.dot(left, right, preferred_element_type=jnp.float32)

        def block(i, q):
            return out[i * GROUP : (i + 1) * GROUP, q * parts : (q + 1) * parts]

        for c in range(3):
            moved_out[c, rows] = block(c, 0)
        trace = block(0, 1) + block(1, 2) + block(2, 3)
        bulk = STEP * (lame[rows] * trace)
        twist = (2.0 * STEP) * shear[rows]
        for s, (i, j) in enumerate(SIX):
            if i == j:
                stress_out[s, rows] = stress[s, rows] + (bulk + twist * block(i, j + 1))
            else:
                rate = 0.5 * (block(i, j + 1) + block(j, i + 1))
                stress_out[s, rows] = stress[s, rows] + twist * rate


def on_device(
    velocity,
    particle_mass,
    particle_volume,
    lame_first,
    shear_modulus,
    stress,
    corner_weights,
    corner_grads,
    tile_block,
    face_blocks,
):
    weights, grads = corner_weights[0], corner_grads[:, 0]
    tiles, nodes, parts = weights.shape
    cuts, face_count = face_blocks.shape[1:]
    faces = cuts * face_count
    groups = tiles // GROUP
    vmem = pl.BlockSpec(memory_space=pltpu.VMEM)
    hbm = pl.BlockSpec(memory_space=pl.ANY)
    f32 = jnp.float32
    dma = pltpu.SemaphoreType.DMA
    moved, updated = pl.pallas_call(
        kernel,
        out_shape=(
            jax.ShapeDtypeStruct((3, tiles, parts), f32),
            jax.ShapeDtypeStruct((6, tiles, parts), f32),
        ),
        in_specs=[vmem] * 6 + [hbm] * 2 + [vmem] * 2,
        out_specs=(vmem, vmem),
        scratch_shapes=[
            pltpu.VMEM((tiles, nodes, parts), jnp.bfloat16),
            pltpu.VMEM((3, tiles, nodes, parts), jnp.bfloat16),
            pltpu.VMEM((tiles, 4 * nodes), f32),
            pltpu.VMEM((faces, 4 * nodes), f32),
            pltpu.VMEM((tiles, 4 * nodes), f32),
            pltpu.VMEM((1, tiles), jnp.int32),
            pltpu.VMEM((2, faces, 4 * nodes), f32),
            dma((groups, 2)),
            dma((2,)),
            dma((2,)),
            dma((2, cuts)),
            dma((2, cuts)),
        ],
        compiler_params=pltpu.CompilerParams(collective_id=0, has_side_effects=True),
        name="step",
    )(
        velocity.reshape(3, tiles, parts),
        particle_mass.reshape(tiles, parts),
        particle_volume.reshape(tiles, parts),
        lame_first.reshape(tiles, parts),
        shear_modulus.reshape(tiles, parts),
        stress.reshape(6, tiles, parts),
        weights,
        grads,
        tile_block,
        face_blocks[0],
    )
    return moved.reshape(3, 1, -1), updated.reshape(6, 1, -1)


def solution(mesh):
    in_specs = (
        P(None, "brick", "shard"),
        P("brick", "shard"),
        P("brick", "shard"),
        P("brick", "shard"),
        P("brick", "shard"),
        P(None, "brick", "shard"),
        P("brick", "shard", None, None),
        P(None, "brick", "shard", None, None),
        P("brick", "shard"),
        P("brick", None, None),
    )
    out_specs = (P(None, "brick", "shard"), P(None, "brick", "shard"))
    return jax.shard_map(
        on_device, mesh=mesh, in_specs=in_specs, out_specs=out_specs, check_vma=False
    )
```

```python
import jax
import jax.numpy as jnp
from jax import lax
from jax.experimental import pallas as pl
from jax.experimental.pallas import tpu as pltpu
from jax.sharding import PartitionSpec as P

NB = 256
STEP = 0.5
FLOOR = 1.0
MESH = pl.DeviceIdType.MESH
GROUP = 8
SPANS = 4
VMEM_LIMIT = 16 * 2**20
PAIRING = ((0, 3, 5), (3, 1, 4), (5, 4, 2))
SIX = ((0, 0), (1, 1), (2, 2), (0, 1), (1, 2), (0, 2))


def thirds(value):
    high = value.astype(jnp.bfloat16)
    rest = value - high.astype(jnp.float32)
    middle = rest.astype(jnp.bfloat16)
    low = (rest - middle.astype(jnp.float32)).astype(jnp.bfloat16)
    return jnp.concatenate([high, middle, low], 1)


def select_sum(chosen, value):
    wide = value.shape[1]
    out = jnp.dot(chosen, thirds(value), preferred_element_type=jnp.float32)
    return out[:, :wide] + out[:, wide : 2 * wide] + out[:, 2 * wide :]


def column_of(row):
    size = row.shape[1]
    square = jnp.broadcast_to(row, (size, size))
    rows = lax.broadcasted_iota(jnp.int32, (size, size), 0)
    columns = lax.broadcasted_iota(jnp.int32, (size, size), 1)
    return jnp.sum(jnp.where(rows == columns, square, 0.0), axis=1, keepdims=True)


def row_of(column):
    size = column.shape[0]
    square = jnp.broadcast_to(column, (size, size))
    rows = lax.broadcasted_iota(jnp.int32, (size, size), 0)
    columns = lax.broadcasted_iota(jnp.int32, (size, size), 1)
    return jnp.sum(jnp.where(rows == columns, square, 0.0), axis=0, keepdims=True)


def equal(column, row):
    return jnp.where(column == row, 1.0, 0.0).astype(jnp.bfloat16)


def exchange_kernel(
    velocity_in,
    mass_in,
    volume_in,
    lame_in,
    shear_in,
    stress_in,
    weights_in,
    grads_in,
    blocks_in,
    faces_in,
    speeds_out,
    weights,
    grads,
    stress,
    lame,
    shear,
    velocity,
    mass,
    volume,
    blocks,
    faces,
    own_sums,
    face_sums,
    other_sums,
    other_blocks,
    face_in,
    small_sem,
    load_sem,
    sum_sems,
    block_sems,
    face_send,
    face_recv,
):
    brick = lax.axis_index("brick")
    shard = lax.axis_index("shard")
    tiles, nodes, parts = weights.shape
    cuts, face_count = faces.shape
    groups = tiles // GROUP

    small = []
    for source, target in (
        (mass_in, mass),
        (velocity_in, velocity),
        (volume_in, volume),
        (stress_in, stress),
        (blocks_in, blocks),
        (faces_in, faces),
    ):
        small.append(pltpu.make_async_copy(source, target, small_sem.at[len(small)]))
        small[-1].start()
    loads = []
    for g in range(groups):
        rows = pl.ds(g * GROUP, GROUP)
        pair = (
            pltpu.make_async_copy(weights_in.at[rows], weights.at[rows], load_sem.at[g, 0]),
            pltpu.make_async_copy(grads_in.at[:, rows], grads.at[:, rows], load_sem.at[g, 1]),
        )
        for copy in pair:
            copy.start()
        loads.append(pair)
    late = []
    for source, target in ((lame_in, lame), (shear_in, shear)):
        late.append(
            pltpu.make_async_copy(source, target, small_sem.at[len(small) + len(late)])
        )
        late[-1].start()

    sibling = (brick, 1 - shard)
    partners = []
    for k in range(cuts):
        bit = 2**k
        partner = brick + (1 - 2 * ((brick // bit) % 2)) * bit
        partners.append(((partner, shard), (partner, 1 - shard)))
    barrier = pltpu.get_barrier_semaphore()
    greeted = [sibling] + [device for both in partners for device in both]
    for device in greeted:
        pl.semaphore_signal(barrier, inc=1, device_id=device, device_id_type=MESH)

    lanes = lax.broadcasted_iota(jnp.int32, (GROUP, GROUP * nodes), 1)
    sublanes = lax.broadcasted_iota(jnp.int32, (GROUP, GROUP * nodes), 0)
    own_node = lanes // nodes == sublanes
    width = 2 * nodes

    for copy in small:
        copy.wait()
    block_row = blocks[...].astype(jnp.float32)
    block_column = column_of(block_row)
    face_rows = faces[...].astype(jnp.float32)
    face_column = jnp.concatenate([column_of(face_rows[k : k + 1]) for k in range(cuts)], 0)
    face_row = row_of(face_column)
    face_of_tile = equal(block_column, face_row)
    tile_of_face = equal(face_column, block_row)
    same_here = equal(block_column, block_row)

    first_half = lax.broadcasted_iota(jnp.int32, (GROUP, width), 1) < nodes
    for g in range(groups):
        rows = pl.ds(g * GROUP, GROUP)
        for copy in loads[g]:
            copy.wait()
        m = mass[rows]
        zero = jnp.zeros_like(m)
        columns = [jnp.concatenate([m] + [m * velocity[c, rows] for c in range(3)], 0)]
        vol = volume[rows]
        scaled = [(-STEP) * (vol * stress[s, rows]) for s in range(6)]
        for j in range(3):
            columns.append(jnp.concatenate([zero] + [scaled[PAIRING[i][j]] for i in range(3)], 0))
        left = jnp.concatenate([column.astype(jnp.bfloat16) for column in columns], 1)
        right = jnp.concatenate(
            [weights[rows].reshape(GROUP * nodes, parts)]
            + [grads[j, rows].reshape(GROUP * nodes, parts) for j in range(3)],
            1,
        )
        out = lax.dot_general(
            left, right, (((1,), (1,)), ((), ())), preferred_element_type=jnp.float32
        )
        twice = []
        for c in range(4):
            piece = jnp.where(own_node, out[c * GROUP : (c + 1) * GROUP], 0.0)
            total = piece[:, :width]
            for q in range(1, GROUP // 2):
                total = total + piece[:, q * width : (q + 1) * width]
            twice.append(total + pltpu.roll(total, nodes, 1))
        own_sums[rows, :width] = jnp.where(first_half, twice[0], twice[1])
        own_sums[rows, width:] = jnp.where(first_half, twice[2], twice[3])

    pieces = own_sums[...]
    face_sums[...] = select_sum(tile_of_face, pieces)

    pl.semaphore_wait(barrier, len(greeted))
    copies = [
        pltpu.make_async_remote_copy(
            src_ref=own_sums,
            dst_ref=other_sums,
            send_sem=sum_sems.at[0],
            recv_sem=sum_sems.at[1],
            device_id=sibling,
            device_id_type=MESH,
        ),
        pltpu.make_async_remote_copy(
            src_ref=blocks,
            dst_ref=other_blocks,
            send_sem=block_sems.at[0],
            recv_sem=block_sems.at[1],
            device_id=sibling,
            device_id_type=MESH,
        ),
    ]
    for k in reversed(range(cuts)):
        for r in range(2):
            rows = pl.ds(k * face_count, face_count)
            copies.append(
                pltpu.make_async_remote_copy(
                    src_ref=face_sums.at[rows],
                    dst_ref=face_in.at[r, rows],
                    send_sem=face_send.at[r, k],
                    recv_sem=face_recv.at[r, k],
                    device_id=partners[k][r],
                    device_id_type=MESH,
                )
            )
    for copy in copies:
        copy.start()
    total = select_sum(same_here, pieces)
    for copy in late:
        copy.wait()
    copies[0].wait()
    copies[1].wait()
    same_there = equal(block_column, other_blocks[...].astype(jnp.float32))
    total = total + select_sum(same_there, other_sums[...])
    for copy in copies[2:]:
        copy.wait()
    total = total + select_sum(face_of_tile, face_in[0] + face_in[1])

    half = lax.broadcasted_iota(jnp.int32, (tiles, width), 1) < nodes
    one, two = total[:, :width], total[:, width:]
    one_turned, two_turned = pltpu.roll(one, nodes, 1), pltpu.roll(two, nodes, 1)
    node_mass = jnp.where(half, one, one_turned)
    moment = [
        jnp.where(half, one_turned, one),
        jnp.where(half, two, two_turned),
        jnp.where(half, two_turned, two) - STEP * node_mass,
    ]
    floor = jnp.maximum(node_mass, FLOOR)
    bound = jnp.where(brick == 0, float(NB // 8), 0.0)
    fixed = block_column < bound
    for c in range(3):
        speeds_out[c] = jnp.where(fixed, 0.0, moment[c] / floor)


def return_kernel(
    speeds, weights, grads, stress, lame, shear, moved_out, stress_out, moved, updated, sems
):
    tiles, nodes, parts = weights.shape
    lanes = lax.broadcasted_iota(jnp.int32, (GROUP, GROUP * nodes), 1)
    sublanes = lax.broadcasted_iota(jnp.int32, (GROUP, GROUP * nodes), 0)
    own_node = lanes // nodes == sublanes
    pending = []
    span = tiles // SPANS
    for g in range(tiles // GROUP):
        rows = pl.ds(g * GROUP, GROUP)
        left = jnp.concatenate(
            [
                jnp.where(own_node, jnp.concatenate([speeds[c, rows]] * (GROUP // 2), 1), 0.0)
                for c in range(3)
            ],
            0,
        ).astype(jnp.bfloat16)
        right = jnp.concatenate(
            [weights[rows].reshape(GROUP * nodes, parts)]
            + [grads[j, rows].reshape(GROUP * nodes, parts) for j in range(3)],
            1,
        )
        out = jnp.dot(left, right, preferred_element_type=jnp.float32)

        def block(i, q):
            return out[i * GROUP : (i + 1) * GROUP, q * parts : (q + 1) * parts]

        for c in range(3):
            moved[c, rows] = block(c, 0)
        trace = block(0, 1) + block(1, 2) + block(2, 3)
        bulk = STEP * (lame[rows] * trace)
        twist = (2.0 * STEP) * shear[rows]
        for s, (i, j) in enumerate(SIX):
            if i == j:
                updated[s, rows] = stress[s, rows] + (bulk + twist * block(i, j + 1))
            else:
                rate = 0.5 * (block(i, j + 1) + block(j, i + 1))
                updated[s, rows] = stress[s, rows] + twist * rate
        if (g + 1) * GROUP % span == 0:
            part = pl.ds((g + 1) * GROUP - span, span)
            n = len(pending)
            for q, (source, target) in enumerate(((moved, moved_out), (updated, stress_out))):
                copy = pltpu.make_async_copy(
                    source.at[:, part], target.at[:, part], sems.at[n // 2, q]
                )
                copy.start()
                pending.append(copy)
    for copy in pending:
        copy.wait()


def on_device(
    velocity,
    particle_mass,
    particle_volume,
    lame_first,
    shear_modulus,
    stress,
    corner_weights,
    corner_grads,
    tile_block,
    face_blocks,
):
    weights, grads = corner_weights[0], corner_grads[:, 0]
    tiles, nodes, parts = weights.shape
    cuts, face_count = face_blocks.shape[1:]
    faces = cuts * face_count
    groups = tiles // GROUP
    vmem = pl.BlockSpec(memory_space=pltpu.VMEM)
    hbm = pl.BlockSpec(memory_space=pltpu.HBM)
    f32, bf16 = jnp.float32, jnp.bfloat16
    dma = pltpu.SemaphoreType.DMA
    shaped = jax.ShapeDtypeStruct
    inputs = (
        velocity.reshape(3, tiles, parts),
        particle_mass.reshape(tiles, parts),
        particle_volume.reshape(tiles, parts),
        lame_first.reshape(tiles, parts),
        shear_modulus.reshape(tiles, parts),
        stress.reshape(6, tiles, parts),
        weights,
        grads,
        tile_block,
        face_blocks[0],
    )
    held = pl.pallas_call(
        exchange_kernel,
        out_shape=(
            shaped((3, tiles, 2 * nodes), f32),
            shaped((tiles, nodes, parts), bf16),
            shaped((3, tiles, nodes, parts), bf16),
            shaped((6, tiles, parts), f32),
            shaped((tiles, parts), f32),
            shaped((tiles, parts), f32),
        ),
        in_specs=[hbm] * 10,
        out_specs=[vmem] * 6,
        scratch_shapes=[
            pltpu.VMEM((3, tiles, parts), f32),
            pltpu.VMEM((tiles, parts), f32),
            pltpu.VMEM((tiles, parts), f32),
            pltpu.VMEM((1, tiles), jnp.int32),
            pltpu.VMEM((cuts, face_count), jnp.int32),
            pltpu.VMEM((tiles, 4 * nodes), f32),
            pltpu.VMEM((faces, 4 * nodes), f32),
            pltpu.VMEM((tiles, 4 * nodes), f32),
            pltpu.VMEM((1, tiles), jnp.int32),
            pltpu.VMEM((2, faces, 4 * nodes), f32),
            dma((8,)),
            dma((groups, 2)),
            dma((2,)),
            dma((2,)),
            dma((2, cuts)),
            dma((2, cuts)),
        ],
        compiler_params=pltpu.CompilerParams(
            collective_id=0, has_side_effects=True, vmem_limit_bytes=VMEM_LIMIT
        ),
        name="exchange",
    )(
        *(pltpu.with_memory_space_constraint(x, pltpu.HBM) for x in inputs)
    )
    moved, updated = pl.pallas_call(
        return_kernel,
        out_shape=(shaped((3, tiles, parts), f32), shaped((6, tiles, parts), f32)),
        in_specs=[vmem] * 6,
        out_specs=[hbm] * 2,
        scratch_shapes=[
            pltpu.VMEM((3, tiles, parts), f32),
            pltpu.VMEM((6, tiles, parts), f32),
            dma((SPANS, 2)),
        ],
        compiler_params=pltpu.CompilerParams(vmem_limit_bytes=VMEM_LIMIT),
        name="bring_back",
    )(*held)
    return moved.reshape(3, 1, -1), updated.reshape(6, 1, -1)


def solution(mesh):
    in_specs = (
        P(None, "brick", "shard"),
        P("brick", "shard"),
        P("brick", "shard"),
        P("brick", "shard"),
        P("brick", "shard"),
        P(None, "brick", "shard"),
        P("brick", "shard", None, None),
        P(None, "brick", "shard", None, None),
        P("brick", "shard"),
        P("brick", None, None),
    )
    out_specs = (P(None, "brick", "shard"), P(None, "brick", "shard"))
    return jax.shard_map(
        on_device, mesh=mesh, in_specs=in_specs, out_specs=out_specs, check_vma=False
    )
```

```python
import jax
import jax.numpy as jnp
from jax import lax
from jax.experimental import pallas as pl
from jax.experimental.pallas import tpu as pltpu
from jax.sharding import PartitionSpec as P

NB = 256
STEP = 0.5
FLOOR = 1.0
MESH = pl.DeviceIdType.MESH
GROUP = 8
SPANS = 4
STREAMED = 2
VMEM_LIMIT = 16 * 2**20
PAIRING = ((0, 3, 5), (3, 1, 4), (5, 4, 2))
SIX = ((0, 0), (1, 1), (2, 2), (0, 1), (1, 2), (0, 2))


def thirds(value):
    high = value.astype(jnp.bfloat16)
    rest = value - high.astype(jnp.float32)
    middle = rest.astype(jnp.bfloat16)
    low = (rest - middle.astype(jnp.float32)).astype(jnp.bfloat16)
    return jnp.concatenate([high, middle, low], 1)


def select_sum(chosen, value):
    wide = value.shape[1]
    out = jnp.dot(chosen, thirds(value), preferred_element_type=jnp.float32)
    return out[:, :wide] + out[:, wide : 2 * wide] + out[:, 2 * wide :]


def column_of(row):
    size = row.shape[1]
    square = jnp.broadcast_to(row, (size, size))
    rows = lax.broadcasted_iota(jnp.int32, (size, size), 0)
    columns = lax.broadcasted_iota(jnp.int32, (size, size), 1)
    return jnp.sum(jnp.where(rows == columns, square, 0.0), axis=1, keepdims=True)


def row_of(column):
    size = column.shape[0]
    square = jnp.broadcast_to(column, (size, size))
    rows = lax.broadcasted_iota(jnp.int32, (size, size), 0)
    columns = lax.broadcasted_iota(jnp.int32, (size, size), 1)
    return jnp.sum(jnp.where(rows == columns, square, 0.0), axis=0, keepdims=True)


def equal(column, row):
    return jnp.where(column == row, 1.0, 0.0).astype(jnp.bfloat16)


def side_by_side(weights, grads, rows):
    size = weights[rows].shape
    flat = (size[0] * size[1], size[2])
    parts = [weights[rows].reshape(flat)] + [grads[j, rows].reshape(flat) for j in range(3)]
    return jnp.concatenate(parts, 1)


def exchange_kernel(
    velocity_in,
    mass_in,
    volume_in,
    lame_in,
    shear_in,
    stress_in,
    weights_in,
    grads_in,
    blocks_in,
    faces_in,
    speeds_out,
    weights,
    grads,
    stress,
    lame,
    shear,
    velocity,
    mass,
    volume,
    blocks,
    faces,
    own_sums,
    face_sums,
    other_sums,
    other_blocks,
    face_in,
    small_sem,
    load_sem,
    sum_sems,
    block_sems,
    face_send,
    face_recv,
):
    brick = lax.axis_index("brick")
    shard = lax.axis_index("shard")
    tiles, nodes, parts = weights.shape
    cuts, face_count = faces.shape
    groups = tiles // GROUP

    small = []
    for source, target in (
        (mass_in, mass),
        (velocity_in, velocity),
        (volume_in, volume),
        (stress_in, stress),
        (blocks_in, blocks),
        (faces_in, faces),
    ):
        small.append(pltpu.make_async_copy(source, target, small_sem.at[len(small)]))
        small[-1].start()
    loads = []
    for g in range(groups):
        rows = pl.ds(g * GROUP, GROUP)
        pair = (
            pltpu.make_async_copy(weights_in.at[rows], weights.at[rows], load_sem.at[g, 0]),
            pltpu.make_async_copy(grads_in.at[:, rows], grads.at[:, rows], load_sem.at[g, 1]),
        )
        for copy in pair:
            copy.start()
        loads.append(pair)
    late = []
    for source, target in ((lame_in, lame), (shear_in, shear)):
        late.append(
            pltpu.make_async_copy(source, target, small_sem.at[len(small) + len(late)])
        )
        late[-1].start()

    sibling = (brick, 1 - shard)
    partners = []
    for k in range(cuts):
        bit = 2**k
        partner = brick + (1 - 2 * ((brick // bit) % 2)) * bit
        partners.append(((partner, shard), (partner, 1 - shard)))
    barrier = pltpu.get_barrier_semaphore()
    greeted = [sibling] + [device for both in partners for device in both]
    for device in greeted:
        pl.semaphore_signal(barrier, inc=1, device_id=device, device_id_type=MESH)

    own_node = (
        lax.broadcasted_iota(jnp.int32, (GROUP, GROUP * nodes), 1) // nodes
        == lax.broadcasted_iota(jnp.int32, (GROUP, GROUP * nodes), 0)
    )
    width = 2 * nodes

    for copy in small:
        copy.wait()
    block_row = blocks[...].astype(jnp.float32)
    block_column = column_of(block_row)
    face_rows = faces[...].astype(jnp.float32)
    face_column = jnp.concatenate([column_of(face_rows[k : k + 1]) for k in range(cuts)], 0)
    face_row = row_of(face_column)
    face_of_tile = equal(block_column, face_row)
    tile_of_face = equal(face_column, block_row)
    same_here = equal(block_column, block_row)

    packed = parts // (4 * GROUP)
    lane = lax.broadcasted_iota(jnp.int32, (nodes, parts), 1)
    lane_tile = lane // (4 * GROUP) * GROUP + lane % GROUP
    first_half = lax.broadcasted_iota(jnp.int32, (GROUP, width), 1) < nodes
    for h in range(groups // packed):
        stacked = []
        for g in range(h * packed, (h + 1) * packed):
            rows = pl.ds(g * GROUP, GROUP)
            m = mass[rows]
            zero = jnp.zeros_like(m)
            vol = volume[rows]
            scaled = [(-STEP) * (vol * stress[s, rows]) for s in range(6)]
            columns = [jnp.concatenate([m] + [m * velocity[c, rows] for c in range(3)], 0)]
            for j in range(3):
                columns.append(
                    jnp.concatenate([zero] + [scaled[PAIRING[i][j]] for i in range(3)], 0)
                )
            stacked.append(jnp.concatenate(columns, 1))
        right = jnp.concatenate(stacked, 0).astype(jnp.bfloat16)
        kept = jnp.zeros((nodes, parts), jnp.float32)
        first = h * packed
        for g in range(first, first + packed):
            for copy in loads[g]:
                copy.wait()
        rows = pl.ds(first * GROUP, STREAMED * GROUP)
        sums = lax.dot_general(
            side_by_side(weights, grads, rows),
            right,
            (((1,), (1,)), ((), ())),
            preferred_element_type=jnp.float32,
        )
        for g in range(first + STREAMED, first + packed):
            rows = pl.ds(g * GROUP, GROUP)
            out = lax.dot_general(
                right[(g - first) * 4 * GROUP : (g - first + 1) * 4 * GROUP],
                side_by_side(weights, grads, rows),
                (((1,), (1,)), ((), ())),
                preferred_element_type=jnp.float32,
            )
            twice = []
            for c in range(4):
                piece = jnp.where(own_node, out[c * GROUP : (c + 1) * GROUP], 0.0)
                total = piece[:, :width]
                for q in range(1, GROUP // 2):
                    total = total + piece[:, q * width : (q + 1) * width]
                twice.append(total + pltpu.roll(total, nodes, 1))
            own_sums[rows, :width] = jnp.where(first_half, twice[0], twice[1])
            own_sums[rows, width:] = jnp.where(first_half, twice[2], twice[3])
        for t in range(STREAMED * GROUP):
            kept = jnp.where(lane_tile == t, sums[t * nodes : (t + 1) * nodes], kept)
        turned = jnp.transpose(jnp.concatenate([kept, kept], 0))
        for g in range(STREAMED):
            rows = pl.ds((h * packed + g) * GROUP, GROUP)
            twice = [turned[(4 * g + c) * GROUP : (4 * g + c + 1) * GROUP] for c in range(4)]
            own_sums[rows, :width] = jnp.where(first_half, twice[0], twice[1])
            own_sums[rows, width:] = jnp.where(first_half, twice[2], twice[3])

    pieces = own_sums[...]
    face_sums[...] = select_sum(tile_of_face, pieces)

    pl.semaphore_wait(barrier, len(greeted))
    copies = [
        pltpu.make_async_remote_copy(
            src_ref=own_sums,
            dst_ref=other_sums,
            send_sem=sum_sems.at[0],
            recv_sem=sum_sems.at[1],
            device_id=sibling,
            device_id_type=MESH,
        ),
        pltpu.make_async_remote_copy(
            src_ref=blocks,
            dst_ref=other_blocks,
            send_sem=block_sems.at[0],
            recv_sem=block_sems.at[1],
            device_id=sibling,
            device_id_type=MESH,
        ),
    ]
    for k in reversed(range(cuts)):
        for r in range(2):
            rows = pl.ds(k * face_count, face_count)
            copies.append(
                pltpu.make_async_remote_copy(
                    src_ref=face_sums.at[rows],
                    dst_ref=face_in.at[r, rows],
                    send_sem=face_send.at[r, k],
                    recv_sem=face_recv.at[r, k],
                    device_id=partners[k][r],
                    device_id_type=MESH,
                )
            )
    for copy in copies:
        copy.start()
    total = select_sum(same_here, pieces)
    for copy in late:
        copy.wait()
    copies[0].wait()
    copies[1].wait()
    same_there = equal(block_column, other_blocks[...].astype(jnp.float32))
    total = total + select_sum(same_there, other_sums[...])
    for copy in copies[2:]:
        copy.wait()
    total = total + select_sum(face_of_tile, face_in[0] + face_in[1])

    half = lax.broadcasted_iota(jnp.int32, (tiles, width), 1) < nodes
    one, two = total[:, :width], total[:, width:]
    one_turned, two_turned = pltpu.roll(one, nodes, 1), pltpu.roll(two, nodes, 1)
    node_mass = jnp.where(half, one, one_turned)
    moment = [
        jnp.where(half, one_turned, one),
        jnp.where(half, two, two_turned),
        jnp.where(half, two_turned, two) - STEP * node_mass,
    ]
    inverse = 1.0 / jnp.maximum(node_mass, FLOOR)
    bound = jnp.where(brick == 0, float(NB // 8), 0.0)
    fixed = block_column < bound
    for c in range(3):
        speeds_out[c] = jnp.where(fixed, 0.0, moment[c] * inverse)


def return_kernel(
    speeds, weights, grads, stress, lame, shear, moved_out, stress_out, moved, updated, sems
):
    tiles, nodes, parts = weights.shape
    lanes = lax.broadcasted_iota(jnp.int32, (GROUP, GROUP * nodes), 1)
    sublanes = lax.broadcasted_iota(jnp.int32, (GROUP, GROUP * nodes), 0)
    own_node = lanes // nodes == sublanes
    pending = []
    span = tiles // SPANS
    for g in range(tiles // GROUP):
        rows = pl.ds(g * GROUP, GROUP)
        left = jnp.concatenate(
            [
                jnp.where(own_node, jnp.concatenate([speeds[c, rows]] * (GROUP // 2), 1), 0.0)
                for c in range(3)
            ],
            0,
        ).astype(jnp.bfloat16)
        right = jnp.concatenate(
            [weights[rows].reshape(GROUP * nodes, parts)]
            + [grads[j, rows].reshape(GROUP * nodes, parts) for j in range(3)],
            1,
        )
        out = jnp.dot(left, right, preferred_element_type=jnp.float32)

        def block(i, q):
            return out[i * GROUP : (i + 1) * GROUP, q * parts : (q + 1) * parts]

        for c in range(3):
            moved[c, rows] = block(c, 0)
        trace = block(0, 1) + block(1, 2) + block(2, 3)
        bulk = STEP * (lame[rows] * trace)
        twist = (2.0 * STEP) * shear[rows]
        for s, (i, j) in enumerate(SIX):
            if i == j:
                updated[s, rows] = stress[s, rows] + (bulk + twist * block(i, j + 1))
            else:
                rate = 0.5 * (block(i, j + 1) + block(j, i + 1))
                updated[s, rows] = stress[s, rows] + twist * rate
        if (g + 1) * GROUP % span == 0:
            part = pl.ds((g + 1) * GROUP - span, span)
            n = len(pending)
            for q, (source, target) in enumerate(((moved, moved_out), (updated, stress_out))):
                copy = pltpu.make_async_copy(
                    source.at[:, part], target.at[:, part], sems.at[n // 2, q]
                )
                copy.start()
                pending.append(copy)
    for copy in pending:
        copy.wait()


def on_device(
    velocity,
    particle_mass,
    particle_volume,
    lame_first,
    shear_modulus,
    stress,
    corner_weights,
    corner_grads,
    tile_block,
    face_blocks,
):
    weights, grads = corner_weights[0], corner_grads[:, 0]
    tiles, nodes, parts = weights.shape
    cuts, face_count = face_blocks.shape[1:]
    faces = cuts * face_count
    groups = tiles // GROUP
    vmem = pl.BlockSpec(memory_space=pltpu.VMEM)
    hbm = pl.BlockSpec(memory_space=pltpu.HBM)
    f32, bf16 = jnp.float32, jnp.bfloat16
    dma = pltpu.SemaphoreType.DMA
    shaped = jax.ShapeDtypeStruct
    inputs = (
        velocity.reshape(3, tiles, parts),
        particle_mass.reshape(tiles, parts),
        particle_volume.reshape(tiles, parts),
        lame_first.reshape(tiles, parts),
        shear_modulus.reshape(tiles, parts),
        stress.reshape(6, tiles, parts),
        weights,
        grads,
        tile_block,
        face_blocks[0],
    )
    held = pl.pallas_call(
        exchange_kernel,
        out_shape=(
            shaped((3, tiles, 2 * nodes), f32),
            shaped((tiles, nodes, parts), bf16),
            shaped((3, tiles, nodes, parts), bf16),
            shaped((6, tiles, parts), f32),
            shaped((tiles, parts), f32),
            shaped((tiles, parts), f32),
        ),
        in_specs=[hbm] * 10,
        out_specs=[vmem] * 6,
        scratch_shapes=[
            pltpu.VMEM((3, tiles, parts), f32),
            pltpu.VMEM((tiles, parts), f32),
            pltpu.VMEM((tiles, parts), f32),
            pltpu.VMEM((1, tiles), jnp.int32),
            pltpu.VMEM((cuts, face_count), jnp.int32),
            pltpu.VMEM((tiles, 4 * nodes), f32),
            pltpu.VMEM((faces, 4 * nodes), f32),
            pltpu.VMEM((tiles, 4 * nodes), f32),
            pltpu.VMEM((1, tiles), jnp.int32),
            pltpu.VMEM((2, faces, 4 * nodes), f32),
            dma((8,)),
            dma((groups, 2)),
            dma((2,)),
            dma((2,)),
            dma((2, cuts)),
            dma((2, cuts)),
        ],
        compiler_params=pltpu.CompilerParams(
            collective_id=0, has_side_effects=True, vmem_limit_bytes=VMEM_LIMIT
        ),
        name="exchange",
    )(
        *(pltpu.with_memory_space_constraint(x, pltpu.HBM) for x in inputs)
    )
    moved, updated = pl.pallas_call(
        return_kernel,
        out_shape=(shaped((3, tiles, parts), f32), shaped((6, tiles, parts), f32)),
        in_specs=[vmem] * 6,
        out_specs=[hbm] * 2,
        scratch_shapes=[
            pltpu.VMEM((3, tiles, parts), f32),
            pltpu.VMEM((6, tiles, parts), f32),
            dma((SPANS, 2)),
        ],
        compiler_params=pltpu.CompilerParams(vmem_limit_bytes=VMEM_LIMIT),
        name="bring_back",
    )(*held)
    return moved.reshape(3, 1, -1), updated.reshape(6, 1, -1)


def solution(mesh):
    in_specs = (
        P(None, "brick", "shard"),
        P("brick", "shard"),
        P("brick", "shard"),
        P("brick", "shard"),
        P("brick", "shard"),
        P(None, "brick", "shard"),
        P("brick", "shard", None, None),
        P(None, "brick", "shard", None, None),
        P("brick", "shard"),
        P("brick", None, None),
    )
    out_specs = (P(None, "brick", "shard"), P(None, "brick", "shard"))
    return jax.shard_map(
        on_device, mesh=mesh, in_specs=in_specs, out_specs=out_specs, check_vma=False
    )
```
